32 devices in a mesh: head: 4 (over z), blk: 2 (over y), dp: 4 (over x, core).
Axes of the slice: x: 2, y: 2, z: 4, core: 2. Of those that a mesh axis runs over, the one named last changes fastest.
Arguments:
- tokens: bfloat16 [4, 2048, 640], P('dp', ('head', 'blk')), may hold values from -6 to 6
- rope_ids: int32 [4, 2048], P('dp', ('head', 'blk')), may hold values from 0 to 1023, as said below
- order: int32 [4, 2048], P('dp'), may hold values from 0 to 2047, as said below
- out_grad: bfloat16 [4, 2048, 640], P('dp', ('head', 'blk')), may hold values from -6 to 6
- w_query: bfloat16 [640, 1024], P(('blk', 'dp')), may hold values from -0.25 to 0.25
- w_key: bfloat16 [640, 256], P(('blk', 'dp')), may hold values from -0.25 to 0.25
- w_value: bfloat16 [640, 256], P(('blk', 'dp')), may hold values from -0.25 to 0.25
- w_out: bfloat16 [1024, 640], P(('blk', 'dp')), may hold values from -0.1875 to 0.1875
- w_gate: bfloat16 [640, 2048], P(('blk', 'dp')), may hold values from -0.25 to 0.25
- w_up: bfloat16 [640, 2048], P(('blk', 'dp')), may hold values from -0.25 to 0.25
- w_down: bfloat16 [2048, 640], P(('blk', 'dp')), may hold values from -0.125 to 0.125
- gain_in: bfloat16 [640], P(('blk', 'dp')), may hold values from 0.5 to 1.5
- gain_query: bfloat16 [256], P(('blk', 'dp')), may hold values from 0.5 to 1.5
- gain_key: bfloat16 [256], P(('blk', 'dp')), may hold values from 0.5 to 1.5
- gain_attn: bfloat16 [640], P(('blk', 'dp')), may hold values from 0.5 to 1.5
- gain_pre: bfloat16 [640], P(('blk', 'dp')), may hold values from 0.5 to 1.5
- gain_post: bfloat16 [640], P(('blk', 'dp')), may hold values from 0.5 to 1.5
Outputs:
- block_out: bfloat16 [4, 2048, 640], P('dp', ('head', 'blk'))
- grad_tokens: float32 [4, 2048, 640], P('dp', ('head', 'blk'))
- grad_w_query: float32 [640, 1024], P(('blk', 'dp'))
- grad_w_key: float32 [640, 256], P(('blk', 'dp'))
- grad_w_value: float32 [640, 256], P(('blk', 'dp'))
- grad_w_out: float32 [1024, 640], P(('blk', 'dp'))
- grad_w_gate: float32 [640, 2048], P(('blk', 'dp'))
- grad_w_up: float32 [640, 2048], P(('blk', 'dp'))
- grad_w_down: float32 [2048, 640], P(('blk', 'dp'))
- grad_gain_in: float32 [640], P(('blk', 'dp'))
- grad_gain_query: float32 [256], P(('blk', 'dp'))
- grad_gain_key: float32 [256], P(('blk', 'dp'))
- grad_gain_attn: float32 [640], P(('blk', 'dp'))
- grad_gain_pre: float32 [640], P(('blk', 'dp'))
- grad_gain_post: float32 [640], P(('blk', 'dp'))
The draws below stay inside these ranges and needn't reach their ends.
Inputs may be any that keep to these rules, and one draw needn't show every extreme that they name: `order`: each sequence's rows hold every position once; the 256 rows of one device are two runs of 128 consecutive positions, the block numbered c followed by the block numbered 2 * 8 - 1 - c, with c drawn anew for each device and sequence. `rope_ids`: each sequence is a pack of documents; a document begins at every position that is a multiple of min(1024, 1024) and at some others after the first such run; a row's id is its position minus the first position of its document.
All inputs are finite; a program needn't handle non-finite values.
Results may differ from the reference program's by a relative error of at most 0.022.
Values may be sent and summed in bfloat16 or wider, within the bound.
No kernel may reach another device: no remote copies, remote signals or barrier semaphores. Data moves between devices by JAX's collectives and lax.ppermute only.
A program may use at most 128 MiB of HBM per device.

```python
import jax
import jax.numpy as jnp
from jax import lax

D = 640
HEADS = 4
HEAD_DIM = 256
FF = 2048
SEG = 256
SEQS = 4
LEN = 2048


def folded_order(key):
    groups = LEN // SEG
    half_seg = SEG // 2
    seq_keys = jax.random.split(jax.random.fold_in(key, 11), SEQS)
    slot_pairs = jax.vmap(lambda seq_key: jax.random.permutation(seq_key, groups))(seq_keys).astype(jnp.int32)
    offsets = jnp.arange(SEG, dtype=jnp.int32)
    first_half = slot_pairs[:, :, None] * half_seg + offsets[None, None, :]
    second = (2 * groups - 1 - slot_pairs[:, :, None]) * half_seg + offsets[None, None, :] - half_seg
    return jnp.where(offsets[None, None, :] < half_seg, first_half, second).reshape(SEQS, LEN).astype(jnp.int32)


def draw_order(key, part):
    return folded_order(key)


def draw_rope_ids(key, part):
    stored = folded_order(key)
    doc_most = min(1024, LEN // 2)
    positions = jnp.arange(LEN, dtype=jnp.int32)
    starts = jax.random.randint(jax.random.fold_in(key, 12), (SEQS, LEN), 0, 256) == 0
    starts = starts & (positions[None, :] >= doc_most)
    starts = starts | (positions[None, :] % doc_most == 0)
    doc_begin = lax.cummax(jnp.where(starts, positions[None, :], 0), axis=1)
    within = positions[None, :] - doc_begin
    return jnp.take_along_axis(within, stored, axis=1).astype(jnp.int32)


def block_scale(key, extent, shards, smallest, high):
    factor_of, own = 1.0, jax.random.fold_in(key, 6)
    for axis_at, shards_of in shards:
        heights = jnp.exp(jax.random.uniform(jax.random.fold_in(own, axis_at), (shards_of,), jnp.float32, smallest / len(shards), high / len(shards)))
        factor_of = factor_of * jnp.repeat(heights, extent[axis_at] // shards_of).reshape([-1 if axis == axis_at else 1 for axis in range(len(extent))])
    return factor_of


def scatter_about(own_key, extent, spread, limit, cuts=(), kind=jnp.bfloat16):
    array = spread * jax.random.normal(own_key, extent, jnp.float32)
    if cuts:
        array = array * block_scale(own_key, extent, cuts, -0.22, 0.18)
    return jnp.clip(array, -limit, limit).astype(kind)


def setup_inputs(seed: int = 0) -> dict:
    key_of = jax.random.split(jax.random.key(seed), 18)
    return {
        "tokens": scatter_about(key_of[0], (SEQS, LEN, D), 1.0, 6.0, ((0, 4), (1, 8))),
        "rope_ids": draw_rope_ids(jax.random.fold_in(key_of[17], 71), 0),
        "order": draw_order(jax.random.fold_in(key_of[17], 71), 0),
        "out_grad": scatter_about(key_of[3], (SEQS, LEN, D), 1.0, 6.0, ((0, 4), (1, 8))),
        "w_query": scatter_about(key_of[4], (D, HEADS * HEAD_DIM), D ** -0.5, 0.25, ((0, 8),)),
        "w_key": scatter_about(key_of[5], (D, HEAD_DIM), D ** -0.5, 0.25, ((0, 8),)),
        "w_value": scatter_about(key_of[6], (D, HEAD_DIM), D ** -0.5, 0.25, ((0, 8),)),
        "w_out": scatter_about(key_of[7], (HEADS * HEAD_DIM, D), (HEADS * HEAD_DIM) ** -0.5, 0.1875, ((0, 8),)),
        "w_gate": scatter_about(key_of[8], (D, FF), D ** -0.5, 0.25, ((0, 8),)),
        "w_up": scatter_about(key_of[9], (D, FF), D ** -0.5, 0.25, ((0, 8),)),
        "w_down": scatter_about(key_of[10], (FF, D), FF ** -0.5, 0.125, ((0, 8),)),
        "gain_in": jnp.clip(1.0 + 0.1 * jax.random.normal(key_of[11], (D,), jnp.float32), 0.5, 1.5).astype(jnp.bfloat16),
        "gain_query": jnp.clip(1.0 + 0.1 * jax.random.normal(key_of[12], (HEAD_DIM,), jnp.float32), 0.5, 1.5).astype(jnp.bfloat16),
        "gain_key": jnp.clip(1.0 + 0.1 * jax.random.normal(key_of[13], (HEAD_DIM,), jnp.float32), 0.5, 1.5).astype(jnp.bfloat16),
        "gain_attn": jnp.clip(1.0 + 0.1 * jax.random.normal(key_of[14], (D,), jnp.float32), 0.5, 1.5).astype(jnp.bfloat16),
        "gain_pre": jnp.clip(1.0 + 0.1 * jax.random.normal(key_of[15], (D,), jnp.float32), 0.5, 1.5).astype(jnp.bfloat16),
        "gain_post": jnp.clip(1.0 + 0.1 * jax.random.normal(key_of[16], (D,), jnp.float32), 0.5, 1.5).astype(jnp.bfloat16),
    }


@jax.custom_vjp
def low(v):
    return lax.optimization_barrier(v.astype(jnp.bfloat16)).astype(jnp.float32)

@jax.custom_vjp
def low_back(v):
    return v

def low_keep(v):
    return (low(v), None)

def low_pass(kept, grad):
    return (grad,)

def back_keep(v):
    return (v, None)

def back_low(kept, grad):
    return (low(grad),)
low.defvjp(low_keep, low_pass)
low_back.defvjp(back_keep, back_low)
NORM_EPSILON = 1e-06
ROPE_BASE = 1000000.0
PRECISE = lax.Precision.HIGHEST

def rms_scale(values, gain_vec):
    return values * lax.rsqrt(lax.optimization_barrier(jnp.mean(values * values, axis=-1, keepdims=True)) + NORM_EPSILON) * gain_vec

def rope_tables(positions, head_width):
    half_width = head_width // 2
    frequency = ROPE_BASE ** (-2.0 * jnp.arange(half_width, dtype=jnp.float32) / head_width)
    angles = positions.astype(jnp.float32)[:, None] * frequency[None, :]
    angles = jnp.concatenate([angles, angles], axis=-1)
    return (jnp.cos(angles), jnp.sin(angles))

def rotate(values, cosine, sine_table):
    half_width = values.shape[-1] // 2
    turned = jnp.concatenate([-values[..., half_width:], values[..., :half_width]], axis=-1)
    return values * cosine + turned * sine_table

def product(left_side, right_side):
    return jnp.dot(left_side, right_side, precision=PRECISE)

def sequence_layer(tokens, positions, order_row, weights):
    w_query, w_key, w_value, w_out, w_gate, w_up, w_down, gain_in, gain_query, gain_key, gain_attn, gain_pre, gain_post = weights
    length = tokens.shape[0]
    cosine, sine_table = rope_tables(positions, HEAD_DIM)
    normed = low(rms_scale(tokens, gain_in))
    query_raw = low_back(product(normed, w_query))
    key_raw = low_back(product(normed, w_key))
    value_raw = low_back(product(normed, w_value))
    query_rot = rotate(rms_scale(query_raw.reshape(length, HEADS, HEAD_DIM), gain_query), cosine[:, None, :], sine_table[:, None, :])
    query_rot = low(query_rot)
    key_rot = low(rotate(rms_scale(key_raw, gain_key), cosine, sine_table))
    value_low = low(value_raw)
    block_rows = min(512, length)
    query_blocks = query_rot.reshape(length // block_rows, block_rows, HEADS, HEAD_DIM)
    order_blocks = order_row.reshape(length // block_rows, block_rows)

    def attend(block_item):
        query_block, query_order = block_item
        scores = jnp.einsum('qhd,kd->hqk', query_block, key_rot, precision=PRECISE) * HEAD_DIM ** (-0.5)
        scores = low_back(scores)
        visible = order_row[None, None, :] <= query_order[None, :, None]
        attn_probs = jax.nn.softmax(jnp.where(visible, scores, -1e+30), axis=-1)
        mixture = jnp.einsum('hqk,kd->qhd', low(attn_probs), value_low, precision=PRECISE)
        return low_back(low(mixture)).reshape(block_rows, HEADS * HEAD_DIM)
    attended = lax.map(jax.checkpoint(attend), (query_blocks, order_blocks)).reshape(length, HEADS * HEAD_DIM)
    out_raw = low_back(product(attended, w_out))
    middle = tokens + rms_scale(out_raw, gain_attn)
    pre_ffn = low(rms_scale(middle, gain_pre))
    gate_proj = low_back(product(pre_ffn, w_gate))
    up_proj = low_back(product(pre_ffn, w_up))
    hidden = low(jax.nn.gelu(gate_proj, approximate=True) * up_proj)
    ffn_out = low_back(product(hidden, w_down))
    return middle + rms_scale(ffn_out, gain_post)

def reference(tokens, rope_ids, order, out_grad, w_query, w_key, w_value, w_out, w_gate, w_up, w_down, gain_in, gain_query, gain_key, gain_attn, gain_pre, gain_post):
    weights = tuple((member.astype(jnp.float32) for member in (w_query, w_key, w_value, w_out, w_gate, w_up, w_down, gain_in, gain_query, gain_key, gain_attn, gain_pre, gain_post)))

    def whole_layer(inputs, params):
        return lax.map(lambda block_item: sequence_layer(block_item[0], block_item[1], block_item[2], params), (inputs, rope_ids, order))
    outputs, pullback = jax.vjp(whole_layer, tokens.astype(jnp.float32), weights)
    grad_tokens, weight_grads = pullback(out_grad.astype(jnp.float32))
    return (outputs.astype(jnp.bfloat16), grad_tokens, weight_grads[0], weight_grads[1], weight_grads[2], weight_grads[3], weight_grads[4], weight_grads[5], weight_grads[6], weight_grads[7], weight_grads[8], weight_grads[9], weight_grads[10], weight_grads[11], weight_grads[12])
```

```python
import functools

import jax
import jax.numpy as jnp
from jax import lax
from jax.experimental import pallas as pl
from jax.experimental.pallas import tpu as pltpu
from jax.sharding import PartitionSpec as P

NORM_EPSILON = 1e-06
ROPE_BASE = 1000000.0
MASKED = -1e30
F32 = jnp.float32
BF16 = jnp.bfloat16


FLIPS = {
    "core": ("dp", [(i, i ^ 1) for i in range(4)]),
    "x": ("dp", [(i, i ^ 2) for i in range(4)]),
    "y": ("blk", [(i, i ^ 1) for i in range(2)]),
}
LINE_IN = [(0, 1), (3, 2)]
LINE_MID = [(1, 2), (2, 1)]
LINE_OUT = [(1, 0), (2, 3)]
RING = [(0, 1), (1, 3), (3, 2), (2, 0)]
RING_SOURCE = ((0, 1, 2, 3), (2, 0, 3, 1), (3, 2, 1, 0), (1, 3, 0, 2))


def flip(array, kind):
    axis, pairs = FLIPS[kind]
    return lax.ppermute(array, axis, pairs)


def rms_scale(values, gain_vec):
    return (
        values
        * lax.rsqrt(jnp.mean(values * values, axis=-1, keepdims=True) + NORM_EPSILON)
        * gain_vec
    )


def rope_tables(positions, head_width):
    half_width = head_width // 2
    frequency = ROPE_BASE ** (-2.0 * jnp.arange(half_width, dtype=F32) / head_width)
    angles = positions.astype(F32)[:, None] * frequency[None, :]
    cosine, sine = jnp.cos(angles), jnp.sin(angles)
    return (
        jnp.concatenate([cosine, cosine], axis=-1),
        jnp.concatenate([sine, sine], axis=-1),
    )


def rotate(values, cosine, sine_table):
    half_width = values.shape[-1] // 2
    turned = jnp.concatenate([-values[..., half_width:], values[..., :half_width]], axis=-1)
    return values * cosine + turned * sine_table


def gated_gelu(gate_in, up_in):
    return jax.nn.gelu(gate_in, approximate=True) * up_in


def plain_dot(left_side, right_side):
    return jnp.dot(left_side, right_side, preferred_element_type=F32)


def contract_rows(left_side, right_side):
    return lax.dot_general(
        left_side, right_side, (((0,), (0,)), ((), ())), preferred_element_type=F32
    )


def contract_cols(left_side, right_side):
    return lax.dot_general(
        left_side, right_side, (((1,), (1,)), ((), ())), preferred_element_type=F32
    )


def attend_kernel(heads, dim, q_ref, kv_ref, kord_ref, qord_ref, o_ref, lse_ref, m_ref, l_ref, acc_ref):
    step = pl.program_id(0)

    @pl.when(step == 0)
    def _():
        m_ref[...] = jnp.full_like(m_ref, MASKED)
        l_ref[...] = jnp.zeros_like(l_ref)
        acc_ref[...] = jnp.zeros_like(acc_ref)

    key = kv_ref[:, :dim]
    value = kv_ref[:, dim:]
    visible = kord_ref[...] <= qord_ref[...]
    scale = dim ** (-0.5)
    for h in range(heads):
        scores = contract_cols(key, q_ref[:, h * dim : (h + 1) * dim]) * scale
        scores = jnp.where(visible, scores, MASKED)
        old = m_ref[h : h + 1, :]
        new = jnp.maximum(old, jnp.max(scores, axis=0, keepdims=True))
        weights = jnp.where(visible, jnp.exp(scores - new), 0.0)
        factor = jnp.exp(old - new)
        m_ref[h : h + 1, :] = new
        l_ref[h : h + 1, :] = l_ref[h : h + 1, :] * factor + jnp.sum(weights, axis=0, keepdims=True)
        acc_ref[h] = acc_ref[h] * factor + contract_rows(value, weights.astype(BF16))

    @pl.when(step == pl.num_programs(0) - 1)
    def _():
        lse_ref[...] = m_ref[...] + jnp.log(l_ref[...])
        for h in range(heads):
            o_ref[:, h * dim : (h + 1) * dim] = (acc_ref[h] / l_ref[h : h + 1, :]).T.astype(BF16)


def attend(query, kv, key_order, query_order, dim, key_rows):
    rows, width = query.shape
    heads = width // dim
    length = kv.shape[0]
    whole = lambda *shape: pl.BlockSpec(shape, lambda j: (0,) * len(shape))
    return pl.pallas_call(
        functools.partial(attend_kernel, heads, dim),
        grid=(length // key_rows,),
        out_shape=(
            jax.ShapeDtypeStruct((rows, width), BF16),
            jax.ShapeDtypeStruct((heads, rows), F32),
        ),
        in_specs=[
            whole(rows, width),
            pl.BlockSpec((key_rows, 2 * dim), lambda j: (j, 0)),
            pl.BlockSpec((key_rows, 1), lambda j: (j, 0)),
            whole(1, rows),
        ],
        out_specs=(whole(rows, width), whole(heads, rows)),
        scratch_shapes=[
            pltpu.VMEM((heads, rows), F32),
            pltpu.VMEM((heads, rows), F32),
            pltpu.VMEM((heads, dim, rows), F32),
        ],
        name="attend",
    )(query, kv, key_order[:, None], query_order[None, :])


def attend_back_kernel(
    heads, dim, q_ref, do_ref, kv_ref, kord_ref, qord_ref, lse_ref, delta_ref, dq_ref, dkv_ref
):
    step = pl.program_id(0)

    @pl.when(step == 0)
    def _():
        dq_ref[...] = jnp.zeros_like(dq_ref)

    key = kv_ref[:, :dim]
    value = kv_ref[:, dim:]
    visible = kord_ref[...] <= qord_ref[...]
    scale = dim ** (-0.5)
    key_grad = jnp.zeros(key.shape, F32)
    value_grad = jnp.zeros(key.shape, F32)
    for h in range(heads):
        cols = slice(h * dim, (h + 1) * dim)
        query, out_grad = q_ref[:, cols], do_ref[:, cols]
        scores = contract_cols(key, query) * scale
        weights = jnp.where(visible, jnp.exp(scores - lse_ref[h : h + 1, :]), 0.0)
        prob_grad = contract_cols(value, out_grad)
        score_grad = (weights * (prob_grad - delta_ref[h : h + 1, :])).astype(BF16)
        value_grad = value_grad + plain_dot(weights.astype(BF16), out_grad)
        key_grad = key_grad + plain_dot(score_grad, query)
        dq_ref[:, cols] += contract_rows(score_grad, key) * scale
    dkv_ref[:, :dim] = (key_grad * scale).astype(BF16)
    dkv_ref[:, dim:] = value_grad.astype(BF16)


def attend_back(query, out_grad, kv, key_order, query_order, lse, delta, dim, key_rows):
    rows, width = query.shape
    heads = width // dim
    length = kv.shape[0]
    whole = lambda *shape: pl.BlockSpec(shape, lambda j: (0,) * len(shape))
    return pl.pallas_call(
        functools.partial(attend_back_kernel, heads, dim),
        grid=(length // key_rows,),
        out_shape=(
            jax.ShapeDtypeStruct((rows, width), F32),
            jax.ShapeDtypeStruct((length, 2 * dim), BF16),
        ),
        in_specs=[
            whole(rows, width),
            whole(rows, width),
            pl.BlockSpec((key_rows, 2 * dim), lambda j: (j, 0)),
            pl.BlockSpec((key_rows, 1), lambda j: (j, 0)),
            whole(1, rows),
            whole(heads, rows),
            whole(heads, rows),
        ],
        out_specs=(
            whole(rows, width),
            pl.BlockSpec((key_rows, 2 * dim), lambda j: (j, 0)),
        ),
        name="attend_back",
    )(query, out_grad, kv, key_order[:, None], query_order[None, :], lse, delta)


class WideTransfers:
    def __init__(self, order_row):
        self.order_row = order_row

    def weights(self, w_query, w_key, w_value, w_out, w_gate, w_up, w_down, dim):
        half = w_query.shape[1] // 2
        every = lambda array: lax.all_gather(array, ("blk", "dp"), axis=0, tiled=True)
        first = every(jnp.concatenate([w_query[:, :half], w_key], axis=1))
        second = every(jnp.concatenate([w_query[:, half:], w_value], axis=1))
        return first, second, every(w_out), every(w_gate), every(w_up), every(w_down)

    def gains(self, packed):
        return lax.all_gather(packed, ("blk", "dp"), axis=0, tiled=True)

    def gather_kv(self, kv):
        return lax.all_gather(kv, ("head", "blk"), axis=0, tiled=True), self.order_row

    def scatter_kv(self, kv_grad):
        return lax.psum_scatter(kv_grad, ("head", "blk"), scatter_dimension=0, tiled=True)

    def arrange(self, left):
        return left

    def reduce(self, left, right, colour):
        partial = contract_rows(left, right).astype(BF16)
        return lax.psum_scatter(partial, ("blk", "dp"), scatter_dimension=0, tiled=True)

    def reduce_gains(self, packed):
        return lax.psum_scatter(packed, ("blk", "dp"), scatter_dimension=0, tiled=True)

    def head_sum(self, array):
        return lax.psum(array, "head")


def assemble_kernel(me_ref, sa_ref, ra_ref, sb_ref, rb_ref, a_ref, b_ref):
    relative = pl.program_id(0) ^ me_ref[0]

    @pl.when(relative % 2 == 0)
    def _():
        a_ref[...] = sa_ref[...]
        b_ref[...] = sb_ref[...]

    @pl.when(relative % 2 == 1)
    def _():
        a_ref[...] = ra_ref[...]
        b_ref[...] = rb_ref[...]


def arrange_kernel(rows, me_ref, left_ref, send_ref, keep_ref):
    for place in range(4):
        relative = 2 * (place // 2) + 4 * (place % 2)
        for target, core in ((send_ref, 1), (keep_ref, 0)):
            start = pl.multiple_of(((relative + core) ^ me_ref[0]) * rows, 16)
            target[place * rows : (place + 1) * rows, :] = left_ref[pl.ds(start, rows), :]


class PairTransfers:
    def __init__(self, order_row):
        self.order_row = order_row
        self.me = lax.axis_index("blk") * 4 + lax.axis_index("dp")
        self.me_array = self.me.astype(jnp.int32)[None]

    def spread(self, own, first, second):
        pair = jnp.concatenate([own, flip(own, first)], axis=0)
        four = jnp.concatenate([pair, flip(pair, second)], axis=0)
        return four, flip(four, "core")

    def assemble(self, first, second):
        rows_a, cols_a = first[0].shape[0] // 4, first[0].shape[1]
        rows_b, cols_b = second[0].shape[0] // 4, second[0].shape[1]
        place_a = lambda a, me: ((a ^ me[0]) >> 1, 0)
        place_b = lambda a, me: ((((a ^ me[0]) >> 2) & 1) + 2 * (((a ^ me[0]) >> 1) & 1), 0)
        return pl.pallas_call(
            assemble_kernel,
            grid_spec=pltpu.PrefetchScalarGridSpec(
                num_scalar_prefetch=1,
                grid=(8,),
                in_specs=[
                    pl.BlockSpec((rows_a, cols_a), place_a),
                    pl.BlockSpec((rows_a, cols_a), place_a),
                    pl.BlockSpec((rows_b, cols_b), place_b),
                    pl.BlockSpec((rows_b, cols_b), place_b),
                ],
                out_specs=(
                    pl.BlockSpec((rows_a, cols_a), lambda a, me: (a, 0)),
                    pl.BlockSpec((rows_b, cols_b), lambda a, me: (a, 0)),
                ),
            ),
            out_shape=(
                jax.ShapeDtypeStruct((8 * rows_a, cols_a), BF16),
                jax.ShapeDtypeStruct((8 * rows_b, cols_b), BF16),
            ),
            name="assemble",
        )(self.me_array, *first, *second)

    def weights(self, w_query, w_key, w_value, w_out, w_gate, w_up, w_down, dim):
        half = w_query.shape[1] // 2
        first = self.spread(jnp.concatenate([w_query[:, :half], w_key], axis=1), "x", "y")
        second = self.spread(jnp.concatenate([w_query[:, half:], w_value], axis=1), "y", "x")
        query_key, query_value = self.assemble(first, second)
        out_mat, down_mat = self.assemble(self.spread(w_out, "x", "y"), self.spread(w_down, "y", "x"))
        gate_mat, up_mat = self.assemble(self.spread(w_gate, "x", "y"), self.spread(w_up, "y", "x"))
        return query_key, query_value, out_mat, gate_mat, up_mat, down_mat

    def gains(self, packed):
        four, other = self.spread(packed, "x", "y")
        relative = jnp.stack([four, other], axis=1).reshape(8, packed.shape[1])
        return jnp.take(relative, jnp.arange(8) ^ self.me, axis=0)

    def gather_kv(self, kv):
        rows = kv.shape[0]
        head, blk = lax.axis_index("head"), lax.axis_index("blk")
        parts, orders = [], []
        held = kv
        for step in range(4):
            parts += [held, flip(held, "y")]
            source = jnp.array(RING_SOURCE[step], jnp.int32)[head]
            for side in (blk, 1 - blk):
                orders.append(
                    lax.dynamic_slice_in_dim(self.order_row, (source * 2 + side) * rows, rows)
                )
            if step < 3:
                held = lax.ppermute(held, "head", RING)
        return jnp.concatenate(parts, axis=0), jnp.concatenate(orders)

    def scatter_kv(self, kv_grad):
        rows = kv_grad.shape[0] // 8
        piece = lambda k, side: kv_grad[(2 * k + side) * rows : (2 * k + side + 1) * rows]
        total = None
        for k in (1, 2, 3, 0):
            mine = piece(k, 0).astype(F32) + flip(piece(k, 1), "y").astype(F32)
            if total is not None:
                mine = mine + total.astype(F32)
            if k:
                total = lax.ppermute(mine.astype(BF16), "head", RING)
        return mine

    def arrange(self, left):
        left_t = left.T
        rows = left_t.shape[0] // 8
        half = jax.ShapeDtypeStruct((4 * rows, left_t.shape[1]), left.dtype)
        return pl.pallas_call(
            functools.partial(arrange_kernel, rows),
            in_specs=[
                pl.BlockSpec(memory_space=pltpu.SMEM),
                pl.BlockSpec(memory_space=pltpu.VMEM),
            ],
            out_specs=(
                pl.BlockSpec(memory_space=pltpu.VMEM),
                pl.BlockSpec(memory_space=pltpu.VMEM),
            ),
            out_shape=(half, half),
            name="arrange",
        )(self.me_array, left_t)

    def reduce(self, left, right, colour):
        send, keep = left
        got = flip(plain_dot(send, right).astype(BF16), "core")
        total = (plain_dot(keep, right) + got.astype(F32)).astype(BF16)
        rows, cols = total.shape[0] // 4, total.shape[1]
        total = total.reshape(2, 2, rows, cols)
        if colour == "x":
            away, stay, later = total[1], total[0], "y"
        else:
            away, stay, later = total[:, 1], total[:, 0], "x"
        got = flip(away, colour)
        away = (stay[1].astype(F32) + got[1].astype(F32)).astype(BF16)
        stay = (stay[0].astype(F32) + got[0].astype(F32)).astype(BF16)
        return (stay.astype(F32) + flip(away, later).astype(F32)).astype(BF16)

    def reduce_gains(self, packed):
        total = jnp.take(packed, jnp.arange(8) ^ self.me, axis=0).reshape(2, 2, 2, -1)
        total = total[:, :, 0] + flip(total[:, :, 1], "core")
        total = total[:, 0] + flip(total[:, 1], "x")
        return total[:1] + flip(total[1:], "y")

    def head_sum(self, array):
        wide = lambda v: v.astype(F32)
        total = (wide(array) + wide(lax.ppermute(array, "head", LINE_IN))).astype(array.dtype)
        total = (wide(total) + wide(lax.ppermute(total, "head", LINE_MID))).astype(array.dtype)
        head = lax.axis_index("head")
        middle = (head == 1) | (head == 2)
        return jnp.where(middle, total, lax.ppermute(total, "head", LINE_OUT))


def local(
    pairwise,
    tokens,
    rope_ids,
    order,
    out_grad,
    w_query,
    w_key,
    w_value,
    w_out,
    w_gate,
    w_up,
    w_down,
    gain_in,
    gain_query,
    gain_key,
    gain_attn,
    gain_pre,
    gain_post,
):
    order_row = order[0]
    moves = PairTransfers(order_row) if pairwise else WideTransfers(order_row)
    seg_rows, width = tokens.shape[1:]
    dim = w_key.shape[1]
    heads = w_query.shape[1] // dim
    half = heads * dim // 2
    wide_part, head_part = gain_in.shape[0], gain_query.shape[0]
    key_rows = min(512, 2 * seg_rows)

    packed = jnp.concatenate(
        [gain_in, gain_attn, gain_pre, gain_post, gain_query, gain_key]
    )[None]
    gains = moves.gains(packed).astype(F32)
    cut = lambda at, size: gains[:, at : at + size].reshape(-1)
    in_gain, attn_gain, pre_gain, post_gain = (cut(i * wide_part, wide_part) for i in range(4))
    query_gain, key_gain = (cut(4 * wide_part + i * head_part, head_part) for i in range(2))
    query_key_mat, query_value_mat, out_mat, gate_mat, up_mat, down_mat = moves.weights(
        w_query, w_key, w_value, w_out, w_gate, w_up, w_down, dim
    )

    device_at = lax.axis_index("head") * lax.axis_size("blk") + lax.axis_index("blk")
    query_order = lax.dynamic_slice_in_dim(order_row, device_at * seg_rows, seg_rows)
    inputs = tokens[0].astype(F32)
    cosine, sine_table = rope_tables(rope_ids[0], dim)
    normed = rms_scale(inputs, in_gain).astype(BF16)
    first_raw = plain_dot(normed, query_key_mat)
    second_raw = plain_dot(normed, query_value_mat)
    query_raw = jnp.concatenate([first_raw[:, :half], second_raw[:, :half]], axis=1)
    key_raw, value_raw = first_raw[:, half:], second_raw[:, half:]

    def rotate_both(query_in, key_in, query_scale, key_scale):
        shaped = query_in.reshape(seg_rows, heads, dim)
        query_out = rotate(
            rms_scale(shaped, query_scale), cosine[:, None, :], sine_table[:, None, :]
        )
        key_out = rotate(rms_scale(key_in, key_scale), cosine, sine_table)
        return (query_out.reshape(seg_rows, heads * dim), key_out)

    query_rot, key_rot = rotate_both(query_raw, key_raw, query_gain, key_gain)
    query_low = query_rot.astype(BF16)
    kv = jnp.concatenate([key_rot.astype(BF16), value_raw.astype(BF16)], axis=1)
    kv_all, key_order = moves.gather_kv(kv)
    attn_rows, lse = attend(query_low, kv_all, key_order, query_order, dim, key_rows)

    out_raw = plain_dot(attn_rows, out_mat)
    middle = inputs + rms_scale(out_raw, attn_gain)
    pre_ffn = rms_scale(middle, pre_gain).astype(BF16)
    gate_proj = plain_dot(pre_ffn, gate_mat)
    up_proj = plain_dot(pre_ffn, up_mat)
    hidden = gated_gelu(gate_proj, up_proj).astype(BF16)
    ffn_out = plain_dot(hidden, down_mat)
    block_out = middle + rms_scale(ffn_out, post_gain)

    cotangent = out_grad[0].astype(F32)
    unused, post_back = jax.vjp(rms_scale, ffn_out, post_gain)
    ffn_grad, post_gain_grad = post_back(cotangent)
    ffn_grad = ffn_grad.astype(BF16)
    down_part = moves.reduce(moves.arrange(hidden), ffn_grad, "y")
    hidden_grad = contract_cols(ffn_grad, down_mat)
    unused, glu_back = jax.vjp(gated_gelu, gate_proj, up_proj)
    gate_grad, up_grad = glu_back(hidden_grad)
    gate_grad = gate_grad.astype(BF16)
    up_grad = up_grad.astype(BF16)
    pre_sides = moves.arrange(pre_ffn)
    gate_part = moves.reduce(pre_sides, gate_grad, "x")
    up_part = moves.reduce(pre_sides, up_grad, "y")
    pre_grad = contract_cols(gate_grad, gate_mat) + contract_cols(up_grad, up_mat)
    unused, pre_back = jax.vjp(rms_scale, middle, pre_gain)
    middle_part, pre_gain_grad = pre_back(pre_grad)
    middle_grad = cotangent + middle_part
    unused, attn_back = jax.vjp(rms_scale, out_raw, attn_gain)
    out_raw_grad, attn_gain_grad = attn_back(middle_grad)
    out_raw_grad = out_raw_grad.astype(BF16)
    out_part = moves.reduce(moves.arrange(attn_rows), out_raw_grad, "x")
    attn_grad = contract_cols(out_raw_grad, out_mat).astype(BF16)
    row_delta = jnp.sum(
        (attn_grad.astype(F32) * attn_rows.astype(F32)).reshape(seg_rows, heads, dim), axis=2
    ).T

    query_grad, kv_partial = attend_back(
        query_low, attn_grad, kv_all, key_order, query_order, lse, row_delta, dim, key_rows
    )
    kv_grad = moves.scatter_kv(kv_partial).astype(F32)
    key_grad, value_grad = kv_grad[:, :dim], kv_grad[:, dim:]
    unused, rotate_back = jax.vjp(rotate_both, query_raw, key_raw, query_gain, key_gain)
    query_raw_grad, key_raw_grad, query_gain_grad, key_gain_grad = rotate_back(
        (query_grad, key_grad)
    )
    first_grad = jnp.concatenate([query_raw_grad[:, :half], key_raw_grad], axis=1).astype(BF16)
    second_grad = jnp.concatenate([query_raw_grad[:, half:], value_grad], axis=1).astype(BF16)
    normed_sides = moves.arrange(normed)
    first_part = moves.reduce(normed_sides, first_grad, "x")
    second_part = moves.reduce(normed_sides, second_grad, "y")
    normed_grad = contract_cols(first_grad, query_key_mat) + contract_cols(
        second_grad, query_value_mat
    )
    unused, in_back = jax.vjp(rms_scale, inputs, in_gain)
    input_part, in_gain_grad = in_back(normed_grad)
    input_grad = middle_grad + input_part

    gain_grads = jnp.concatenate(
        [g.reshape(-1, wide_part) for g in (in_gain_grad, attn_gain_grad, pre_gain_grad, post_gain_grad)]
        + [g.reshape(-1, head_part) for g in (query_gain_grad, key_gain_grad)],
        axis=1,
    )
    gain_sums = moves.head_sum(moves.reduce_gains(gain_grads))[0]
    gain_cut = lambda at, size: gain_sums[at : at + size]
    sums = [
        moves.head_sum(part).astype(F32)
        for part in (first_part, second_part, out_part, gate_part, up_part, down_part)
    ]
    first_sum, second_sum, out_sum, gate_sum, up_sum, down_sum = sums
    return (
        block_out.astype(BF16)[None],
        input_grad[None],
        jnp.concatenate([first_sum[:, :half], second_sum[:, :half]], axis=1),
        first_sum[:, half:],
        second_sum[:, half:],
        out_sum,
        gate_sum,
        up_sum,
        down_sum,
        gain_cut(0, wide_part),
        gain_cut(4 * wide_part, head_part),
        gain_cut(4 * wide_part + head_part, head_part),
        gain_cut(wide_part, wide_part),
        gain_cut(2 * wide_part, wide_part),
        gain_cut(3 * wide_part, wide_part),
    )


def solution(mesh):
    sizes = mesh.shape
    pairwise = sizes["head"] == 4 and sizes["blk"] == 2 and sizes["dp"] == 4
    rows3 = P("dp", ("head", "blk"), None)
    matrix, vector = P(("blk", "dp"), None), P(("blk", "dp"))
    return jax.shard_map(
        functools.partial(local, pairwise),
        mesh=mesh,
        in_specs=(rows3, P("dp", ("head", "blk")), P("dp", None), rows3)
        + (matrix,) * 7
        + (vector,) * 6,
        out_specs=(rows3, rows3) + (matrix,) * 7 + (vector,) * 6,
        check_vma=False,
    )
```

```python
import functools

import jax
import jax.numpy as jnp
from jax import lax
from jax.experimental import pallas as pl
from jax.experimental.pallas import tpu as pltpu
from jax.sharding import PartitionSpec as P

NORM_EPSILON = 1e-06
ROPE_BASE = 1000000.0
MASKED = -1e30
F32 = jnp.float32
BF16 = jnp.bfloat16


FLIPS = {
    "core": ("dp", [(i, i ^ 1) for i in range(4)]),
    "x": ("dp", [(i, i ^ 2) for i in range(4)]),
    "y": ("blk", [(i, i ^ 1) for i in range(2)]),
}
LINE_IN = [(0, 1), (3, 2)]
LINE_MID = [(1, 2), (2, 1)]
LINE_OUT = [(1, 0), (2, 3)]
RING = [(0, 1), (1, 3), (3, 2), (2, 0)]
RING_SOURCE = ((0, 1, 2, 3), (2, 0, 3, 1), (3, 2, 1, 0), (1, 3, 0, 2))


def flip(array, kind):
    axis, pairs = FLIPS[kind]
    return lax.ppermute(array, axis, pairs)


def rms_scale(values, gain_vec):
    return (
        values
        * lax.rsqrt(jnp.mean(values * values, axis=-1, keepdims=True) + NORM_EPSILON)
        * gain_vec
    )


def rope_tables(positions, head_width):
    half_width = head_width // 2
    frequency = ROPE_BASE ** (-2.0 * jnp.arange(half_width, dtype=F32) / head_width)
    angles = positions.astype(F32)[:, None] * frequency[None, :]
    cosine, sine = jnp.cos(angles), jnp.sin(angles)
    return (
        jnp.concatenate([cosine, cosine], axis=-1),
        jnp.concatenate([sine, sine], axis=-1),
    )


def rotate(values, cosine, sine_table):
    half_width = values.shape[-1] // 2
    turned = jnp.concatenate([-values[..., half_width:], values[..., :half_width]], axis=-1)
    return values * cosine + turned * sine_table


def gated_gelu(gate_in, up_in):
    return jax.nn.gelu(gate_in, approximate=True) * up_in


def plain_dot(left_side, right_side):
    return jnp.dot(left_side, right_side, preferred_element_type=F32)


def contract_rows(left_side, right_side):
    return lax.dot_general(
        left_side, right_side, (((0,), (0,)), ((), ())), preferred_element_type=F32
    )


def contract_cols(left_side, right_side):
    return lax.dot_general(
        left_side, right_side, (((1,), (1,)), ((), ())), preferred_element_type=F32
    )


def attend_kernel(heads, dim, q_ref, kv_ref, kord_ref, qord_ref, o_ref, lse_ref, m_ref, l_ref, acc_ref):
    step = pl.program_id(0)

    @pl.when(step == 0)
    def _():
        m_ref[...] = jnp.full_like(m_ref, MASKED)
        l_ref[...] = jnp.zeros_like(l_ref)
        acc_ref[...] = jnp.zeros_like(acc_ref)

    key = kv_ref[:, :dim]
    value = kv_ref[:, dim:]
    visible = kord_ref[...] <= qord_ref[...]
    scale = dim ** (-0.5)
    for h in range(heads):
        scores = contract_cols(key, q_ref[:, h * dim : (h + 1) * dim]) * scale
        scores = jnp.where(visible, scores, MASKED)
        old = m_ref[h : h + 1, :]
        new = jnp.maximum(old, jnp.max(scores, axis=0, keepdims=True))
        weights = jnp.where(visible, jnp.exp(scores - new), 0.0)
        factor = jnp.exp(old - new)
        m_ref[h : h + 1, :] = new
        l_ref[h : h + 1, :] = l_ref[h : h + 1, :] * factor + jnp.sum(weights, axis=0, keepdims=True)
        acc_ref[h] = acc_ref[h] * factor + contract_rows(value, weights.astype(BF16))

    @pl.when(step == pl.num_programs(0) - 1)
    def _():
        lse_ref[...] = m_ref[...] + jnp.log(l_ref[...])
        for h in range(heads):
            o_ref[:, h * dim : (h + 1) * dim] = (acc_ref[h] / l_ref[h : h + 1, :]).T.astype(BF16)


def attend(query, kv, key_order, query_order, dim, key_rows):
    rows, width = query.shape
    heads = width // dim
    length = kv.shape[0]
    whole = lambda *shape: pl.BlockSpec(shape, lambda j: (0,) * len(shape))
    return pl.pallas_call(
        functools.partial(attend_kernel, heads, dim),
        grid=(length // key_rows,),
        out_shape=(
            jax.ShapeDtypeStruct((rows, width), BF16),
            jax.ShapeDtypeStruct((heads, rows), F32),
        ),
        in_specs=[
            whole(rows, width),
            pl.BlockSpec((key_rows, 2 * dim), lambda j: (j, 0)),
            pl.BlockSpec((key_rows, 1), lambda j: (j, 0)),
            whole(1, rows),
        ],
        out_specs=(whole(rows, width), whole(heads, rows)),
        scratch_shapes=[
            pltpu.VMEM((heads, rows), F32),
            pltpu.VMEM((heads, rows), F32),
            pltpu.VMEM((heads, dim, rows), F32),
        ],
        name="attend",
    )(query, kv, key_order[:, None], query_order[None, :])


def attend_back_kernel(
    heads, dim, q_ref, do_ref, kv_ref, kord_ref, qord_ref, lse_ref, delta_ref, dq_ref, dkv_ref
):
    step = pl.program_id(0)

    @pl.when(step == 0)
    def _():
        dq_ref[...] = jnp.zeros_like(dq_ref)

    key = kv_ref[:, :dim]
    value = kv_ref[:, dim:]
    visible = kord_ref[...] <= qord_ref[...]
    scale = dim ** (-0.5)
    key_grad = jnp.zeros(key.shape, F32)
    value_grad = jnp.zeros(key.shape, F32)
    for h in range(heads):
        cols = slice(h * dim, (h + 1) * dim)
        query, out_grad = q_ref[:, cols], do_ref[:, cols]
        scores = contract_cols(key, query) * scale
        weights = jnp.where(visible, jnp.exp(scores - lse_ref[h : h + 1, :]), 0.0)
        prob_grad = contract_cols(value, out_grad)
        score_grad = (weights * (prob_grad - delta_ref[h : h + 1, :])).astype(BF16)
        value_grad = value_grad + plain_dot(weights.astype(BF16), out_grad)
        key_grad = key_grad + plain_dot(score_grad, query)
        dq_ref[:, cols] += contract_rows(score_grad, key) * scale
    dkv_ref[:, :dim] = (key_grad * scale).astype(BF16)
    dkv_ref[:, dim:] = value_grad.astype(BF16)


def attend_back(query, out_grad, kv, key_order, query_order, lse, delta, dim, key_rows):
    rows, width = query.shape
    heads = width // dim
    length = kv.shape[0]
    whole = lambda *shape: pl.BlockSpec(shape, lambda j: (0,) * len(shape))
    return pl.pallas_call(
        functools.partial(attend_back_kernel, heads, dim),
        grid=(length // key_rows,),
        out_shape=(
            jax.ShapeDtypeStruct((rows, width), F32),
            jax.ShapeDtypeStruct((length, 2 * dim), BF16),
        ),
        in_specs=[
            whole(rows, width),
            whole(rows, width),
            pl.BlockSpec((key_rows, 2 * dim), lambda j: (j, 0)),
            pl.BlockSpec((key_rows, 1), lambda j: (j, 0)),
            whole(1, rows),
            whole(heads, rows),
            whole(heads, rows),
        ],
        out_specs=(
            whole(rows, width),
            pl.BlockSpec((key_rows, 2 * dim), lambda j: (j, 0)),
        ),
        name="attend_back",
    )(query, out_grad, kv, key_order[:, None], query_order[None, :], lse, delta)


def rms_back(grad, values, root, gain_vec):
    inner = jnp.mean(values * gain_vec * grad, axis=-1, keepdims=True)
    back = root * gain_vec * grad - values * (root * root * root) * inner
    return back, jnp.sum(grad * values * root, axis=0, keepdims=True)


def root_of(values):
    return lax.rsqrt(jnp.mean(values * values, axis=-1, keepdims=True) + NORM_EPSILON)


def middle_kernel(
    sizes,
    me_ref,
    attn_ref,
    tokens_ref,
    cot_ref,
    gains_ref,
    gate_s,
    gate_r,
    up_s,
    up_r,
    od_s,
    od_r,
    block_ref,
    middle_grad_ref,
    attn_grad_ref,
    delta_ref,
    gain_grad_ref,
    gate_send,
    gate_keep,
    up_send,
    up_keep,
    od_send,
    od_keep,
    gate_w,
    up_w,
    out_w,
    down_w,
    gate_p,
    up_p,
    hidden,
    gate_g,
    up_g,
    pre_t,
    pre_rel,
    sems,
):
    parts, chunk, dim = sizes
    me = me_ref[0]
    in_rows = gate_w.shape[0] // parts
    out_rows = out_w.shape[0] // parts
    down_rows = down_w.shape[0] // parts
    both_rows = out_rows + down_rows
    ff = gate_w.shape[1]
    chunks = [slice(c, c + chunk) for c in range(0, ff, chunk)]

    def piece(kind, block, place, source):
        start = lambda rows, extra=0: pl.multiple_of(place * rows + extra, 16)
        if kind == 0:
            src, dst = source[0].at[pl.ds(start(both_rows), out_rows)], out_w.at[pl.ds(block * out_rows, out_rows)]
        elif kind == 1:
            src, dst = source[1].at[pl.ds(start(in_rows), in_rows)], gate_w.at[pl.ds(block * in_rows, in_rows)]
        elif kind == 2:
            src, dst = source[2].at[pl.ds(start(in_rows), in_rows)], up_w.at[pl.ds(block * in_rows, in_rows)]
        else:
            src, dst = (
                source[0].at[pl.ds(start(both_rows, out_rows), down_rows)],
                down_w.at[pl.ds(block * down_rows, down_rows)],
            )
        return pltpu.make_async_copy(src, dst, sems.at[kind, block])

    for kind in range(4):
        for block in range(parts):
            relative = block ^ me
            by_x = relative >> 1
            by_y = ((relative >> 2) & 1) + 2 * ((relative >> 1) & 1)
            place = by_x if kind == 1 else by_y

            @pl.when((relative & 1) == 0)
            def _():
                piece(kind, block, place, (od_s, gate_s, up_s)).start()

            @pl.when((relative & 1) == 1)
            def _():
                piece(kind, block, place, (od_r, gate_r, up_r)).start()

    def ready(kind):
        for block in range(parts):
            piece(kind, block, 0, (od_s, gate_s, up_s)).wait()

    attn_gain, pre_gain, post_gain = (gains_ref[i : i + 1, :] for i in range(3))
    ready(0)
    out_raw = plain_dot(attn_ref[...], out_w[...])
    out_root = root_of(out_raw)
    middle = tokens_ref[...].astype(F32) + out_raw * out_root * attn_gain
    middle_root = root_of(middle)
    pre = (middle * middle_root * pre_gain).astype(BF16)
    ready(1)
    ready(2)
    for cols in chunks:
        gate = plain_dot(pre, gate_w[:, cols])
        up = plain_dot(pre, up_w[:, cols])
        gate_p[:, cols] = gate
        up_p[:, cols] = up
        hidden[:, cols] = gated_gelu(gate, up).astype(BF16)
    ready(3)
    ffn_out = plain_dot(hidden[...], down_w[...])
    ffn_root = root_of(ffn_out)
    block_ref[...] = (middle + ffn_out * ffn_root * post_gain).astype(BF16)
    cotangent = cot_ref[...].astype(F32)
    ffn_grad, gain_grad_ref[2:3, :] = rms_back(cotangent, ffn_out, ffn_root, post_gain)
    ffn_grad = ffn_grad.astype(BF16)
    curve = (2.0 / jnp.pi) ** 0.5
    for cols in chunks:
        hidden_grad = contract_cols(ffn_grad, down_w[cols, :])
        gate, up = gate_p[:, cols], up_p[:, cols]
        bent = jnp.tanh(curve * (gate + 0.044715 * (gate * gate * gate)))
        half_on = 0.5 * (1.0 + bent)
        slope = half_on + 0.5 * gate * (1.0 - bent * bent) * curve * (1.0 + 0.134145 * (gate * gate))
        gate_g[:, cols] = (hidden_grad * up * slope).astype(BF16)
        up_g[:, cols] = (hidden_grad * (gate * half_on)).astype(BF16)
    pre_grad = contract_cols(gate_g[...], gate_w[...]) + contract_cols(up_g[...], up_w[...])
    middle_part, gain_grad_ref[1:2, :] = rms_back(pre_grad, middle, middle_root, pre_gain)
    middle_grad = cotangent + middle_part
    middle_grad_ref[...] = middle_grad
    out_grad, gain_grad_ref[0:1, :] = rms_back(middle_grad, out_raw, out_root, attn_gain)
    out_grad = out_grad.astype(BF16)
    attn_grad = contract_cols(out_grad, out_w[...]).astype(BF16)
    attn_grad_ref[...] = attn_grad
    for h in range(attn_grad.shape[1] // dim):
        cols = slice(h * dim, (h + 1) * dim)
        product = attn_grad[:, cols].astype(F32) * attn_ref[:, cols].astype(F32)
        delta_ref[h : h + 1, :] = jnp.sum(product.T, axis=0, keepdims=True)

    pre_t[...] = pre.T
    for core in range(2):
        for place in range(4):
            relative = core + 2 * (place // 2) + 4 * (place % 2)
            source = pl.multiple_of((relative ^ me) * in_rows, 16)
            target = ((1 - core) * 4 + place) * in_rows
            pre_rel[target : target + in_rows, :] = pre_t[pl.ds(source, in_rows), :]
    sides = 4 * in_rows
    for cols in chunks:
        gate_send[:, cols] = plain_dot(pre_rel[:sides, :], gate_g[:, cols]).astype(BF16)
        gate_keep[:, cols] = plain_dot(pre_rel[sides:, :], gate_g[:, cols]).astype(BF16)
        up_send[:, cols] = plain_dot(pre_rel[:sides, :], up_g[:, cols]).astype(BF16)
        up_keep[:, cols] = plain_dot(pre_rel[sides:, :], up_g[:, cols]).astype(BF16)
    for core, target in ((1, od_send), (0, od_keep)):
        for place in range(4):
            relative = core + 2 * (place // 2) + 4 * (place % 2)
            block = relative ^ me
            left = attn_ref[:, pl.ds(pl.multiple_of(block * out_rows, 128), out_rows)]
            low = place * both_rows
            target[low : low + out_rows, :] = contract_rows(left, out_grad).astype(BF16)
            left = hidden[:, pl.ds(pl.multiple_of(block * down_rows, 128), down_rows)]
            target[low + out_rows : low + both_rows, :] = contract_rows(left, ffn_grad).astype(BF16)


def middle_pass(me_array, attn_rows, tokens, cotangent, gains3, gate, up, both, out_rows, dim):
    rows, width = tokens.shape
    parts = 8
    in_rows, ff = gate[0].shape[0] // 4, gate[0].shape[1]
    both_rows = both[0].shape[0] // 4
    down_rows = both_rows - out_rows
    heads = attn_rows.shape[1] // dim
    vmem = pl.BlockSpec(memory_space=pltpu.VMEM)
    anywhere = pl.BlockSpec(memory_space=pl.ANY)
    shape = jax.ShapeDtypeStruct
    return pl.pallas_call(
        functools.partial(middle_kernel, (parts, min(512, ff), dim)),
        in_specs=[pl.BlockSpec(memory_space=pltpu.SMEM)] + [vmem] * 4 + [anywhere] * 6,
        out_specs=(vmem,) * 11,
        out_shape=(
            shape((rows, width), BF16),
            shape((rows, width), F32),
            shape(attn_rows.shape, BF16),
            shape((heads, rows), F32),
            shape((8, width), F32),
            shape((4 * in_rows, ff), BF16),
            shape((4 * in_rows, ff), BF16),
            shape((4 * in_rows, ff), BF16),
            shape((4 * in_rows, ff), BF16),
            shape((4 * both_rows, width), BF16),
            shape((4 * both_rows, width), BF16),
        ),
        scratch_shapes=[
            pltpu.VMEM((parts * in_rows, ff), BF16),
            pltpu.VMEM((parts * in_rows, ff), BF16),
            pltpu.VMEM((parts * out_rows, width), BF16),
            pltpu.VMEM((parts * down_rows, width), BF16),
            pltpu.VMEM((rows, ff), F32),
            pltpu.VMEM((rows, ff), F32),
            pltpu.VMEM((rows, ff), BF16),
            pltpu.VMEM((rows, ff), BF16),
            pltpu.VMEM((rows, ff), BF16),
            pltpu.VMEM((parts * in_rows, rows), BF16),
            pltpu.VMEM((parts * in_rows, rows), BF16),
            pltpu.SemaphoreType.DMA((4, parts)),
        ],
        name="middle",
    )(me_array, attn_rows, tokens, cotangent, gains3, *gate, *up, *both)


def middle_plain(moves, attn_rows, tokens, out_grad, gains3, mats, dim):
    attn_gain, pre_gain, post_gain = gains3
    out_mat, gate_mat, up_mat, down_mat = mats
    inputs, cotangent = tokens.astype(F32), out_grad.astype(F32)
    out_raw = plain_dot(attn_rows, out_mat)
    middle = inputs + rms_scale(out_raw, attn_gain)
    pre_ffn = rms_scale(middle, pre_gain).astype(BF16)
    gate_proj = plain_dot(pre_ffn, gate_mat)
    up_proj = plain_dot(pre_ffn, up_mat)
    hidden = gated_gelu(gate_proj, up_proj).astype(BF16)
    ffn_out = plain_dot(hidden, down_mat)
    block_out = middle + rms_scale(ffn_out, post_gain)
    unused, post_back = jax.vjp(rms_scale, ffn_out, post_gain)
    ffn_grad, post_gain_grad = post_back(cotangent)
    ffn_grad = ffn_grad.astype(BF16)
    hidden_grad = contract_cols(ffn_grad, down_mat)
    unused, glu_back = jax.vjp(gated_gelu, gate_proj, up_proj)
    gate_grad, up_grad = (g.astype(BF16) for g in glu_back(hidden_grad))
    pre_grad = contract_cols(gate_grad, gate_mat) + contract_cols(up_grad, up_mat)
    unused, pre_back = jax.vjp(rms_scale, middle, pre_gain)
    middle_part, pre_gain_grad = pre_back(pre_grad)
    middle_grad = cotangent + middle_part
    unused, attn_back = jax.vjp(rms_scale, out_raw, attn_gain)
    out_raw_grad, attn_gain_grad = attn_back(middle_grad)
    out_raw_grad = out_raw_grad.astype(BF16)
    attn_grad = contract_cols(out_raw_grad, out_mat).astype(BF16)
    row_delta = jnp.sum(
        (attn_grad.astype(F32) * attn_rows.astype(F32)).reshape(tokens.shape[0], -1, dim), axis=2
    ).T
    parts = (
        moves.reduce(pre_ffn, gate_grad),
        moves.reduce(pre_ffn, up_grad),
        moves.reduce(attn_rows, out_raw_grad),
        moves.reduce(hidden, ffn_grad),
    )
    gain_grads = (attn_gain_grad, pre_gain_grad, post_gain_grad)
    return block_out.astype(BF16), middle_grad, attn_grad, row_delta, gain_grads, parts


class WideTransfers:
    def __init__(self, order_row):
        self.order_row = order_row

    def every(self, array):
        return lax.all_gather(array, ("blk", "dp"), axis=0, tiled=True)

    def first_weights(self, first, second, packed):
        return self.every(first), self.every(second), self.every(packed)

    def middle(self, w_out, w_gate, w_up, w_down):
        mats = [self.every(w) for w in (w_out, w_gate, w_up, w_down)]

        def run(attn_rows, tokens, out_grad, gains3, dim):
            return middle_plain(self, attn_rows, tokens, out_grad, gains3, mats, dim)

        return run

    def finish_middle(self, parts, tie):
        sums = [self.head_sum(part).astype(F32) for part in parts]
        return sums, tie

    def gather_kv(self, kv):
        return lax.all_gather(kv, ("head", "blk"), axis=0, tiled=True), self.order_row

    def scatter_kv(self, kv_grad):
        return lax.psum_scatter(kv_grad, ("head", "blk"), scatter_dimension=0, tiled=True)

    def reduce(self, left, right):
        partial = contract_rows(left, right).astype(BF16)
        return lax.psum_scatter(partial, ("blk", "dp"), scatter_dimension=0, tiled=True)

    def finish_first(self, normed, first_grad, second_grad, gain_grads):
        gains = lax.psum_scatter(gain_grads, ("blk", "dp"), scatter_dimension=0, tiled=True)
        return (
            self.head_sum(self.reduce(normed, first_grad)).astype(F32),
            self.head_sum(self.reduce(normed, second_grad)).astype(F32),
            self.head_sum(gains)[0],
        )

    def head_sum(self, array):
        return lax.psum(array, "head")


def assemble_kernel(rows, me_ref, sa_ref, ra_ref, sb_ref, rb_ref, a_ref, b_ref, g_ref):
    relative = pl.program_id(0) ^ me_ref[0]

    @pl.when(relative % 2 == 0)
    def _():
        a_ref[...] = sa_ref[...]
        b_ref[...] = sb_ref[:rows, :]
        g_ref[...] = sb_ref[rows:, :]

    @pl.when(relative % 2 == 1)
    def _():
        a_ref[...] = ra_ref[...]
        b_ref[...] = rb_ref[:rows, :]
        g_ref[...] = rb_ref[rows:, :]


def arrange_kernel(rows, me_ref, left_ref, send_ref, keep_ref):
    for place in range(4):
        relative = 2 * (place // 2) + 4 * (place % 2)
        for target, core in ((send_ref, 1), (keep_ref, 0)):
            start = pl.multiple_of(((relative + core) ^ me_ref[0]) * rows, 16)
            target[place * rows : (place + 1) * rows, :] = left_ref[pl.ds(start, rows), :]


def add(left, right):
    return (left.astype(F32) + right.astype(F32)).astype(BF16)


class PairTransfers:
    def __init__(self, order_row):
        self.order_row = order_row
        self.me = lax.axis_index("blk") * 4 + lax.axis_index("dp")
        self.me_array = self.me.astype(jnp.int32)[None]

    def spread_pair(self, own, first, name):
        with jax.named_scope(name + "_1"):
            return jnp.concatenate([own, flip(own, first)], axis=0)

    def spread_four(self, pair, second, name):
        with jax.named_scope(name + "_2"):
            four = jnp.concatenate([pair, flip(pair, second)], axis=0)
        with jax.named_scope(name + "_3"):
            return four, flip(four, "core")

    def first_weights(self, first, second, packed):
        pad_cols = second.shape[1] - packed.shape[1]
        second = jnp.concatenate([second, jnp.pad(packed, ((0, 7), (0, pad_cols)))], axis=0)
        pair_a = self.spread_pair(first, "x", "ga")
        pair_b = self.spread_pair(second, "y", "gb")
        self.early = (pair_a, pair_b)
        first, second = self.spread_four(pair_a, "y", "ga"), self.spread_four(pair_b, "x", "gb")
        rows, cols = first[0].shape[0] // 4, first[0].shape[1]
        tall = rows + 8
        place_a = lambda a, me: ((a ^ me[0]) >> 1, 0)
        place_b = lambda a, me: ((((a ^ me[0]) >> 2) & 1) + 2 * (((a ^ me[0]) >> 1) & 1), 0)
        out_block = lambda height: pl.BlockSpec((height, cols), lambda a, me: (a, 0))
        first_mat, second_mat, gains = pl.pallas_call(
            functools.partial(assemble_kernel, rows),
            grid_spec=pltpu.PrefetchScalarGridSpec(
                num_scalar_prefetch=1,
                grid=(8,),
                in_specs=[pl.BlockSpec((rows, cols), place_a)] * 2
                + [pl.BlockSpec((tall, cols), place_b)] * 2,
                out_specs=(out_block(rows), out_block(rows), out_block(8)),
            ),
            out_shape=(
                jax.ShapeDtypeStruct((8 * rows, cols), BF16),
                jax.ShapeDtypeStruct((8 * rows, cols), BF16),
                jax.ShapeDtypeStruct((64, cols), BF16),
            ),
            name="assemble",
        )(self.me_array, *first, *second)
        return first_mat, second_mat, gains.reshape(8, 8, cols)[:, 0, : packed.shape[1]]

    def middle(self, w_out, w_gate, w_up, w_down):
        both = jnp.concatenate([w_out, w_down], axis=0)
        both, w_gate, w_up, unused = lax.optimization_barrier((both, w_gate, w_up, self.early))
        both_pair = self.spread_pair(both, "y", "go")
        gate_pair = self.spread_pair(w_gate, "x", "gg")
        up_pair = self.spread_pair(w_up, "y", "gu")
        both = self.spread_four(both_pair, "x", "go")
        gate = self.spread_four(gate_pair, "y", "gg")
        up = self.spread_four(up_pair, "x", "gu")
        out_rows = w_out.shape[0]

        def run(attn_rows, tokens, out_grad, gains3, dim):
            with jax.named_scope("middle_call"):
                results = middle_pass(
                    self.me_array, attn_rows, tokens, out_grad, jnp.stack(gains3),
                    gate, up, both, out_rows, dim,
                )
            block_out, middle_grad, attn_grad, row_delta, gain_grads = results[:5]
            self.out_rows = out_rows
            return block_out, middle_grad, attn_grad, row_delta, tuple(gain_grads[:3]), results[5:]

        return run

    def start_middle(self, parts):
        with jax.named_scope("rs_core"):
            got = [flip(send, "core") for send in parts[0::2]]
        return [
            add(keep, other).reshape(2, 2, keep.shape[0] // 4, keep.shape[1])
            for keep, other in zip(parts[1::2], got)
        ]

    def finish_middle(self, parts, tie):
        totals = self.start_middle(parts)
        after = []
        for at, total in enumerate(totals):
            with jax.named_scope("rs_x%d" % at):
                got = flip(total[1], "x")
            away, stay = add(total[0, 1], got[1]), add(total[0, 0], got[0])
            with jax.named_scope("rs_y%d" % at):
                after.append(add(stay, flip(away, "y")))
        gate, up, both = after
        rows = gate.shape[0]
        wide = self.head_sum(jnp.concatenate([gate, up], axis=0), "hs0").astype(F32)
        both = self.head_sum(both, "hs1").astype(F32)
        return [wide[:rows], wide[rows:], both[: self.out_rows], both[self.out_rows :]], tie

    def gather_kv(self, kv):
        rows = kv.shape[0]
        head, blk = lax.axis_index("head"), lax.axis_index("blk")
        parts, orders = [], []
        held = kv
        for step in range(4):
            with jax.named_scope("kvf_y%d" % step):
                parts += [held, flip(held, "y")]
            source = jnp.array(RING_SOURCE[step], jnp.int32)[head]
            for side in (blk, 1 - blk):
                orders.append(
                    lax.dynamic_slice_in_dim(self.order_row, (source * 2 + side) * rows, rows)
                )
            if step < 3:
                with jax.named_scope("kvf_z%d" % step):
                    held = lax.ppermute(held, "head", RING)
        return jnp.concatenate(parts, axis=0), jnp.concatenate(orders)

    def scatter_kv(self, kv_grad):
        rows = kv_grad.shape[0] // 8
        piece = lambda k, side: kv_grad[(2 * k + side) * rows : (2 * k + side + 1) * rows]
        total = None
        for k in (1, 2, 3, 0):
            with jax.named_scope("kvb_y%d" % k):
                other = flip(piece(k, 1), "y")
            mine = piece(k, 0).astype(F32) + other.astype(F32)
            if total is not None:
                mine = mine + total.astype(F32)
            if k:
                with jax.named_scope("kvb_z%d" % k):
                    total = lax.ppermute(mine.astype(BF16), "head", RING)
        return mine

    def arrange(self, left):
        left_t = left.T
        rows = left_t.shape[0] // 8
        half = jax.ShapeDtypeStruct((4 * rows, left_t.shape[1]), left.dtype)
        vmem = pl.BlockSpec(memory_space=pltpu.VMEM)
        return pl.pallas_call(
            functools.partial(arrange_kernel, rows),
            in_specs=[pl.BlockSpec(memory_space=pltpu.SMEM), vmem],
            out_specs=(vmem, vmem),
            out_shape=(half, half),
            name="arrange",
        )(self.me_array, left_t)

    def finish_first(self, normed, first_grad, second_grad, gain_grads):
        send, keep = self.arrange(normed)
        rows, cols = send.shape[0] // 4, first_grad.shape[1]
        gains = jnp.take(gain_grads, jnp.arange(8) ^ self.me, axis=0).reshape(2, 2, 2, -1)
        gains = gains.transpose(2, 1, 0, 3).reshape(2, 4, 1, -1).astype(BF16)
        gains = jnp.pad(gains, ((0, 0), (0, 0), (0, 7), (0, cols - gains.shape[3])))
        shaped = lambda v: v.reshape(4, rows, cols)
        with jax.named_scope("fs_core"):
            got_a = flip(plain_dot(send, first_grad).astype(BF16), "core")
            got_b = flip(
                jnp.concatenate([shaped(plain_dot(send, second_grad).astype(BF16)), gains[1]], axis=1),
                "core",
            )
        total_a = add(plain_dot(keep, first_grad), got_a).reshape(2, 2, rows, cols)
        total_b = add(
            jnp.concatenate([shaped(plain_dot(keep, second_grad).astype(BF16)), gains[0]], axis=1),
            got_b,
        ).reshape(2, 2, rows + 8, cols)
        with jax.named_scope("fs_1"):
            got_a = flip(total_a[1], "x")
            got_b = flip(total_b[:, 1], "y")
        away_a, away_b = add(total_a[0, 1], got_a[1]), add(total_b[1, 0], got_b[1])
        stay_a, stay_b = add(total_a[0, 0], got_a[0]), add(total_b[0, 0], got_b[0])
        with jax.named_scope("fs_2"):
            sum_a = add(stay_a, flip(away_a, "y"))
            sum_b = add(stay_b, flip(away_b, "x"))
        whole = self.head_sum(jnp.concatenate([sum_a, sum_b], axis=0), "hs2").astype(F32)
        return whole[:rows], whole[rows : 2 * rows], whole[2 * rows]

    def head_sum(self, array, name):
        with jax.named_scope(name + "_in"):
            total = add(array, lax.ppermute(array, "head", LINE_IN))
        with jax.named_scope(name + "_mid"):
            total = add(total, lax.ppermute(total, "head", LINE_MID))
        head = lax.axis_index("head")
        middle = (head == 1) | (head == 2)
        with jax.named_scope(name + "_out"):
            return jnp.where(middle, total, lax.ppermute(total, "head", LINE_OUT))


def local(
    pairwise,
    tokens,
    rope_ids,
    order,
    out_grad,
    w_query,
    w_key,
    w_value,
    w_out,
    w_gate,
    w_up,
    w_down,
    gain_in,
    gain_query,
    gain_key,
    gain_attn,
    gain_pre,
    gain_post,
):
    order_row = order[0]
    moves = PairTransfers(order_row) if pairwise else WideTransfers(order_row)
    seg_rows, width = tokens.shape[1:]
    dim = w_key.shape[1]
    heads = w_query.shape[1] // dim
    half = heads * dim // 2
    wide_part, head_part = gain_in.shape[0], gain_query.shape[0]
    key_rows = min(512, 2 * seg_rows)

    packed = jnp.concatenate(
        [gain_in, gain_attn, gain_pre, gain_post, gain_query, gain_key]
    )[None]
    query_key_mat, query_value_mat, gains = moves.first_weights(
        jnp.concatenate([w_query[:, :half], w_key], axis=1),
        jnp.concatenate([w_query[:, half:], w_value], axis=1),
        packed,
    )
    gains = gains.astype(F32)
    cut = lambda at, size: gains[:, at : at + size].reshape(-1)
    in_gain, attn_gain, pre_gain, post_gain = (cut(i * wide_part, wide_part) for i in range(4))
    query_gain, key_gain = (cut(4 * wide_part + i * head_part, head_part) for i in range(2))
    run_middle = moves.middle(w_out, w_gate, w_up, w_down)

    device_at = lax.axis_index("head") * lax.axis_size("blk") + lax.axis_index("blk")
    query_order = lax.dynamic_slice_in_dim(order_row, device_at * seg_rows, seg_rows)
    inputs = tokens[0].astype(F32)
    cosine, sine_table = rope_tables(rope_ids[0], dim)
    normed = rms_scale(inputs, in_gain).astype(BF16)
    first_raw = plain_dot(normed, query_key_mat)
    second_raw = plain_dot(normed, query_value_mat)
    query_raw = jnp.concatenate([first_raw[:, :half], second_raw[:, :half]], axis=1)
    key_raw, value_raw = first_raw[:, half:], second_raw[:, half:]

    def rotate_both(query_in, key_in, query_scale, key_scale):
        shaped = query_in.reshape(seg_rows, heads, dim)
        query_out = rotate(
            rms_scale(shaped, query_scale), cosine[:, None, :], sine_table[:, None, :]
        )
        key_out = rotate(rms_scale(key_in, key_scale), cosine, sine_table)
        return (query_out.reshape(seg_rows, heads * dim), key_out)

    query_rot, key_rot = rotate_both(query_raw, key_raw, query_gain, key_gain)
    query_low = query_rot.astype(BF16)
    kv = jnp.concatenate([key_rot.astype(BF16), value_raw.astype(BF16)], axis=1)
    kv_all, key_order = moves.gather_kv(kv)
    attn_rows, lse = attend(query_low, kv_all, key_order, query_order, dim, key_rows)

    block_out, middle_grad, attn_grad, row_delta, gain_grads, middle_parts = run_middle(
        attn_rows, tokens[0], out_grad[0], (attn_gain, pre_gain, post_gain), dim
    )
    attn_gain_grad, pre_gain_grad, post_gain_grad = gain_grads

    query_grad, kv_partial = attend_back(
        query_low, attn_grad, kv_all, key_order, query_order, lse, row_delta, dim, key_rows
    )
    middle_sums, kv_partial = moves.finish_middle(middle_parts, kv_partial)
    kv_grad = moves.scatter_kv(kv_partial).astype(F32)
    key_grad, value_grad = kv_grad[:, :dim], kv_grad[:, dim:]
    unused, rotate_back = jax.vjp(rotate_both, query_raw, key_raw, query_gain, key_gain)
    query_raw_grad, key_raw_grad, query_gain_grad, key_gain_grad = rotate_back(
        (query_grad, key_grad)
    )
    first_grad = jnp.concatenate([query_raw_grad[:, :half], key_raw_grad], axis=1).astype(BF16)
    second_grad = jnp.concatenate([query_raw_grad[:, half:], value_grad], axis=1).astype(BF16)
    normed_grad = contract_cols(first_grad, query_key_mat) + contract_cols(
        second_grad, query_value_mat
    )
    unused, in_back = jax.vjp(rms_scale, inputs, in_gain)
    input_part, in_gain_grad = in_back(normed_grad)
    input_grad = middle_grad + input_part

    gain_grads = jnp.concatenate(
        [g.reshape(-1, wide_part) for g in (in_gain_grad, attn_gain_grad, pre_gain_grad, post_gain_grad)]
        + [g.reshape(-1, head_part) for g in (query_gain_grad, key_gain_grad)],
        axis=1,
    )
    first_sum, second_sum, gain_sums = moves.finish_first(
        normed, first_grad, second_grad, gain_grads
    )
    gain_cut = lambda at, size: gain_sums[at : at + size]
    gate_sum, up_sum, out_sum, down_sum = middle_sums
    return (
        block_out[None],
        input_grad[None],
        jnp.concatenate([first_sum[:, :half], second_sum[:, :half]], axis=1),
        first_sum[:, half:],
        second_sum[:, half:],
        out_sum,
        gate_sum,
        up_sum,
        down_sum,
        gain_cut(0, wide_part),
        gain_cut(4 * wide_part, head_part),
        gain_cut(4 * wide_part + head_part, head_part),
        gain_cut(wide_part, wide_part),
        gain_cut(2 * wide_part, wide_part),
        gain_cut(3 * wide_part, wide_part),
    )


def solution(mesh):
    sizes = mesh.shape
    pairwise = sizes["head"] == 4 and sizes["blk"] == 2 and sizes["dp"] == 4
    rows3 = P("dp", ("head", "blk"), None)
    matrix, vector = P(("blk", "dp"), None), P(("blk", "dp"))
    return jax.shard_map(
        functools.partial(local, pairwise),
        mesh=mesh,
        in_specs=(rows3, P("dp", ("head", "blk")), P("dp", None), rows3)
        + (matrix,) * 7
        + (vector,) * 6,
        out_specs=(rows3, rows3) + (matrix,) * 7 + (vector,) * 6,
        check_vma=False,
    )
```
